512 devices in a mesh: pair: 2 (over core), box: 16 (over z_hi, x), tile: 16 (over z_lo, y).
Axes of the slice: x: 4, y: 8, z: 8 (z_hi: 4, z_lo: 2; z = z_hi * 2 + z_lo), core: 2. Of those that a mesh axis runs over, the one named last changes fastest.
Arguments:
- child_maps: bfloat16 [2, 256, 1152, 1152], P('pair', ('box', 'tile')), parts along dimension 1, as said below
- face_order: int32 [16, 2, 6], P('box'), parts along dimension 0, may hold values from 0 to 5, each once within a row
Outputs:
- parent_update: bfloat16 [2, 256, 960, 768], P('pair', ('box', 'tile')), parts along dimension 1
The draws below stay inside these ranges and needn't reach their ends.
There are 16 independent parts, one for each index of `box`. The reference program is written for one: setup_inputs(seed, part) draws one part's arguments, and reference() takes and returns one part's arrays. A program takes and returns all parts, laid end to end along the dimension named above; each array names one. Nothing has to cross between parts.
Inputs may be any that keep to these rules, and one draw needn't show every extreme that they name: Each row of face_order lists every face once: entry 0 is the child's shared face, entries 1 to 5 its exterior faces in parent order. `child_maps`: child maps are dense with independent entries.
All inputs are finite; a program needn't handle non-finite values.
Results may differ from the reference program's by a relative error of at most 0.012.
Values may be sent and summed in bfloat16 or wider, within the bound.
No kernel may reach another device: no remote copies, remote signals or barrier semaphores. Data moves between devices by JAX's collectives and lax.ppermute only.
A program may use at most 64 MiB of HBM per device.

```python
import math
import jax
import jax.numpy as jnp
from jax import lax

FACE = 768
FACES = 6
CF = 2
ITERS = 3
SIDE = 4
PIECE = 192


def draw_child_maps(key, part):
    order_total = FACES * FACE
    key_diag, key_noise = jax.random.split(jax.random.fold_in(key, 17), 2)
    diagonal = jax.random.uniform(key_diag, (2, order_total, 1), jnp.float32, 0.5, 0.8)
    points = jnp.arange(order_total)
    same_face = points[:, None] // FACE == points[None, :] // FACE
    spread = jnp.where(same_face, 0.3, 0.5) / (2.0 * math.sqrt(FACE))
    noise = jax.random.normal(key_noise, (2, order_total, order_total), jnp.float32)
    full_maps = noise * spread + jnp.where(points[:, None] == points[None, :], diagonal, 0.0)
    blocked = full_maps.reshape(2, FACES, SIDE, PIECE, FACES, SIDE, PIECE).transpose(0, 2, 5, 1, 3, 4, 6)
    return blocked.reshape(2, SIDE * SIDE, FACES * PIECE, FACES * PIECE).astype(jnp.bfloat16)


def setup_inputs(seed: int = 0, part: int = 0) -> dict:
    seeds = jax.random.split(jax.random.key(seed), 3)
    part_keys = jax.random.split(jax.random.fold_in(seeds[2], part), 3)
    return {
        "child_maps": draw_child_maps(jax.random.fold_in(jax.random.fold_in(seeds[2], part), 71), part),
        "face_order": jax.vmap(lambda own: jax.random.permutation(own, FACES))(jax.random.split(part_keys[1], 1 * 2)).reshape((1, 2, FACES)).astype(jnp.int32),
    }


def face_block(matrix, row_face, col_face):
    start_row = (row_face * FACE).astype(jnp.int32)
    start_col = (col_face * FACE).astype(jnp.int32)
    return lax.dynamic_slice(matrix, (start_row, start_col), (FACE, FACE))

def reference(child_maps, face_order):
    order_total = FACES * FACE
    full_maps = child_maps.reshape(2, SIDE, SIDE, FACES, PIECE, FACES, PIECE).transpose(0, 3, 1, 4, 5, 2, 6).reshape(2, order_total, order_total)
    face_list = face_order[0]
    shared, columns, exterior = ([], [], [])
    for child in range(2):
        matrix = full_maps[child]
        own_face = face_list[child, 0]
        shared.append(face_block(matrix, own_face, own_face))
        columns.append(jnp.concatenate([face_block(matrix, own_face, face_list[child, 1 + number]) for number in range(CF)], axis=1))
        exterior.append(jnp.concatenate([face_block(matrix, face_list[child, 1 + number], own_face) for number in range(FACES - 1)], axis=0))
    series, coupled = ([], [])
    for child in range(2):
        partner = 1 - child
        powers = jnp.dot(shared[child], shared[partner], preferred_element_type=jnp.float32).astype(jnp.bfloat16)
        current = columns[child]
        for sweep in range(ITERS):
            current = (current.astype(jnp.float32) + jnp.dot(powers, current, preferred_element_type=jnp.float32)).astype(jnp.bfloat16)
            if sweep < ITERS - 1:
                powers = jnp.dot(powers, powers, preferred_element_type=jnp.float32).astype(jnp.bfloat16)
        series.append(current)
        coupled.append(jnp.dot(shared[partner], current, preferred_element_type=jnp.float32).astype(jnp.bfloat16))
    factors = [jnp.concatenate([coupled[0], series[1]], axis=1), jnp.concatenate([series[0], coupled[1]], axis=1)]
    scaling = math.sqrt(FACE)
    updates = jnp.stack([(jnp.dot(exterior[child], factors[child], preferred_element_type=jnp.float32) * scaling).astype(jnp.bfloat16) for child in range(2)])
    blocked = updates.reshape(2, FACES - 1, SIDE, PIECE, 2 * CF, SIDE, PIECE).transpose(0, 2, 5, 1, 3, 4, 6)
    return blocked.reshape(2, SIDE * SIDE, (FACES - 1) * PIECE, 2 * CF * PIECE)
```

```python
import functools
import math

import jax
import jax.numpy as jnp
from jax import lax
from jax.experimental import pallas as pl
from jax.experimental.pallas import tpu as pltpu
from jax.sharding import PartitionSpec as P

FACE = 768
FACES = 6
CF = 2
PIECE = 192
LANES = 128
HALF = PIECE // 2
TILE_ROWS = PIECE + HALF
WIN_ROWS = CF * PIECE * PIECE // LANES
EXT = FACES - 1
EXT_ROWS = EXT * TILE_ROWS


def dot(a, b):
    return jnp.dot(a, b, preferred_element_type=jnp.float32)


def one_hot(condition):
    return jnp.where(condition, 1.0, 0.0).astype(jnp.bfloat16)


def extract_kernel(face, ids, ca, cb, w0a, w0b, w1a, w1b, tile_out, win_out, ext_out):
    pair, tile = ids[0], ids[1]
    odd_col = tile & 1
    shift = 64 * (face[pair, 0] & 1)
    r = lax.broadcasted_iota(jnp.int32, (256, 256), 0)
    c = lax.broadcasted_iota(jnp.int32, (256, 256), 1)
    first = (c < LANES) & (r == c + shift)

    def rest(offset):
        q = c - LANES - offset
        return first | ((q >= 0) & (q < 64) & (r == q + LANES + shift))

    q_top = one_hot(rest(64 * odd_col))
    q_bottom = one_hot(rest(64 * (1 - odd_col)))
    tops, bottoms = [], []
    for m in range(FACES):
        which = face[pair, (m + 1) % FACES]
        start = pl.multiple_of(which * PIECE, PIECE)
        later = pl.multiple_of(which * PIECE + HALF, HALF)
        tops.append(jnp.concatenate([ca[pl.ds(start, HALF), :], cb[pl.ds(start, HALF), :]], axis=1))
        bottoms.append(jnp.concatenate([ca[pl.ds(later, HALF), :], cb[pl.ds(later, HALF), :]], axis=1))
    top = dot(jnp.concatenate(tops, axis=0), q_top)
    bottom = dot(jnp.concatenate(bottoms, axis=0), q_bottom)
    for m in range(FACES):
        rows = slice(m * HALF, (m + 1) * HALF)
        out, base, tail = (ext_out, m * PIECE, EXT * PIECE + m * HALF) if m < EXT else (tile_out, 0, PIECE)
        out[base : base + HALF, :] = top[rows, :LANES].astype(jnp.bfloat16)
        out[base + HALF : base + PIECE, :] = bottom[rows, :LANES].astype(jnp.bfloat16)
        out[tail : tail + HALF, :] = (top[rows, LANES:] + bottom[rows, LANES:]).astype(jnp.bfloat16)
    r = lax.broadcasted_iota(jnp.int32, (256, CF * PIECE), 0)
    c = lax.broadcasted_iota(jnp.int32, (256, CF * PIECE), 1)
    total = None
    for n, (a, b) in enumerate(((w0a, w0b), (w1a, w1b))):
        q = c - n * PIECE
        move = one_hot((q >= 0) & (q < PIECE) & (r == q + 64 * (face[pair, 1 + n] & 1)))
        part = dot(jnp.concatenate([a[...], b[...]], axis=1), move)
        total = part if total is None else total + part
    for n in range(3):
        win_out[n * PIECE : (n + 1) * PIECE, :] = total[:, n * LANES : (n + 1) * LANES].astype(jnp.bfloat16)


def extract(tile, face, ids):
    def column(order, step):
        return lambda g, f, i: (0, (f[i[0], order] * PIECE) // LANES + step)

    def block(order, step):
        return lambda g, f, i: (f[i[0], 0], (f[i[0], order] * PIECE) // LANES + step)

    def whole(rows):
        return pl.BlockSpec((rows, LANES), lambda g, f, i: (0, 0))

    rows = tile.shape[0]
    return pl.pallas_call(
        extract_kernel,
        grid_spec=pltpu.PrefetchScalarGridSpec(
            num_scalar_prefetch=2,
            grid=(1,),
            in_specs=[pl.BlockSpec((rows, LANES), column(0, 0)), pl.BlockSpec((rows, LANES), column(0, 1))]
            + [pl.BlockSpec((PIECE, LANES), block(1 + n, step)) for n in range(CF) for step in range(2)],
            out_specs=[whole(TILE_ROWS), whole(WIN_ROWS), whole(EXT_ROWS)],
        ),
        out_shape=[jax.ShapeDtypeStruct((n, LANES), jnp.bfloat16) for n in (TILE_ROWS, WIN_ROWS, EXT_ROWS)],
        cost_estimate=pl.CostEstimate(flops=4 * 10**8, bytes_accessed=2 * 10**6, transcendentals=0),
        name="extract",
    )(face, ids, *[tile] * 6)


def main_at(index, own_col):
    return pl.multiple_of(LANES * (index ^ own_col), LANES)


def rest_at(index, own_col):
    return pl.multiple_of(4 * LANES + LANES * ((index ^ own_col) >> 1) + 64 * (index & 1), 64)


def swap_halves(x):
    return jnp.concatenate([x[:, 64:], x[:, :64]], axis=1)


OFFSETS = (0, 1, -1, -2, 2, 3, -3, -4)


def place_tile(source, base, target, rests, row, col, own_col):
    lanes = pl.ds(main_at(col, own_col), LANES)
    target[pl.ds(main_at(row, own_col), LANES), lanes] = source[base : base + LANES, :]
    target[pl.ds(rest_at(row, own_col), 64), lanes] = source[base + LANES : base + PIECE, :]
    rests[row, col] = source[base + PIECE : base + TILE_ROWS, :]


def join_rests(target, rests, own_col):
    left = lax.broadcasted_iota(jnp.int32, (HALF, LANES), 1) < 64

    def body(step, carry):
        row, two = step // 2, step % 2
        even, odd = rests[row, 2 * two], rests[row, 2 * two + 1]
        lanes = pl.ds(pl.multiple_of(4 * LANES + LANES * (two ^ (own_col >> 1)), LANES), LANES)
        top = jnp.where(left, even, odd)
        bottom = swap_halves(jnp.where(left, odd, even))
        start = main_at(row, own_col)
        target[pl.ds(start, HALF), lanes] = top
        target[pl.ds(pl.multiple_of(start + HALF, 32), LANES - HALF), lanes] = bottom[: LANES - HALF]
        target[pl.ds(rest_at(row, own_col), 64), lanes] = bottom[LANES - HALF :]
        return carry

    lax.fori_loop(0, 8, body, 0)


def series_kernel(n_lists, ids, *refs):
    lists = refs[:n_lists]
    out, mine, other, rests, power, power2, start_a, total = refs[n_lists:]
    pair, tile = ids[0], ids[1]
    y, z = tile & 7, tile >> 3
    own_col = tile & 3
    own_row = tile >> 2
    step = 1 - 2 * (y & 1)

    def place(target, sources):
        for n, (source, base) in enumerate(sources):
            t = ((y + OFFSETS[n % 8] * step) & 7) + 8 * (z ^ (n // 8))
            place_tile(source, base, target, rests, t >> 2, t & 3, own_col)
        join_rests(target, rests, own_col)

    def place_window(lane_half, sources, target):
        for n, (source, base) in enumerate(sources):
            row = own_row ^ n
            for piece in range(3):
                at = base + piece * PIECE
                lanes = lane_half(piece)
                target[pl.ds(main_at(row, own_col), LANES), lanes] = source[at : at + LANES, :]
                target[pl.ds(rest_at(row, own_col), 64), lanes] = source[at + LANES : at + PIECE, :]

    tile_sources, win_sources = lists_of(lists)
    place(mine, tile_sources[0])
    place(other, tile_sources[1])
    half = CF * PIECE
    my_half = pair * half
    place_window(lambda p: pl.ds(p * LANES, LANES), win_sources[0], start_a)
    place_window(lambda p: pl.ds(pl.multiple_of(half - my_half + p * LANES, LANES), LANES), win_sources[1], total)

    def rows_of(n):
        return pl.ds(pl.multiple_of(n * 256, 256), 256)

    @pl.loop(0, 3)
    def _(n):
        rows = rows_of(n)
        power[rows, :] = dot(other[rows, :], mine[...]).astype(jnp.bfloat16)
        lanes = pl.ds(pl.multiple_of(my_half, LANES), half)
        total[rows, lanes] = dot(other[rows, :], start_a[...]).astype(jnp.bfloat16)

    def add(matrix, source, target):
        @pl.loop(0, 3)
        def _(n):
            rows = rows_of(n)
            target[rows, :] = (source[rows, :].astype(jnp.float32) + dot(matrix[rows, :], source[...])).astype(
                jnp.bfloat16
            )

    def square(source, target):
        @pl.loop(0, 3)
        def _(n):
            rows = rows_of(n)
            target[rows, :] = dot(source[rows, :], source[...]).astype(jnp.bfloat16)

    square(power, power2)
    add(power, total, mine)
    add(power2, mine, other)
    square(power2, power)
    add(power, other, out)


def lists_of(lists):
    (a0, w, y2, w4, z1, z2, y3, y4, z3, z4, px1, px2) = lists
    both = 2 * TILE_ROWS
    own = [(a0, 0), (a0, TILE_ROWS)] + [(x, n * TILE_ROWS) for x in (y2, y3, y4) for n in range(2)]
    far = [(x, n * TILE_ROWS) for x in (z1, z2, z3, z4) for n in range(2)]
    wins = [(w, 0), (w4, 0), (z1, both), (z2, both)]
    sent = both + WIN_ROWS
    p_tiles = [(px1, base + n * TILE_ROWS) for base in (0, sent) for n in range(2)]
    p_tiles += [(px2, n * TILE_ROWS) for n in range(4)]
    p_tiles += [(px1, base + n * TILE_ROWS) for base in (2 * sent, 3 * sent) for n in range(2)]
    p_tiles += [(px2, n * TILE_ROWS) for n in range(4, 8)]
    p_wins = [(px1, n * sent + both) for n in range(4)]
    return (own + far, p_tiles), (wins, p_wins)


def series(ids, lists):
    vmem = pl.BlockSpec(memory_space=pltpu.VMEM)
    square = pltpu.VMEM((FACE, FACE), jnp.bfloat16)
    return pl.pallas_call(
        functools.partial(series_kernel, len(lists)),
        in_specs=[pl.BlockSpec(memory_space=pltpu.SMEM)] + [vmem] * len(lists),
        out_specs=vmem,
        out_shape=jax.ShapeDtypeStruct((FACE, FACE), jnp.bfloat16),
        scratch_shapes=[
            square,
            square,
            pltpu.VMEM((4, 4, HALF, LANES), jnp.bfloat16),
            square,
            square,
            pltpu.VMEM((FACE, CF * PIECE), jnp.bfloat16),
            square,
        ],
        cost_estimate=pl.CostEstimate(flops=6 * 10**9, bytes_accessed=6 * 10**6, transcendentals=0),
        compiler_params=pltpu.CompilerParams(vmem_limit_bytes=40 * 2**20),
        name="series",
    )(ids, *lists)


def update_kernel(ids, e0, e1, e2, e3, factor, out, matrix):
    odd_col = (ids[1] & 1) == 1
    left = (lax.broadcasted_iota(jnp.int32, (HALF, LANES), 1) < 64) ^ odd_col
    main = EXT * PIECE
    for n, e in enumerate((e0, e1, e2, e3)):
        matrix[:, n * LANES : (n + 1) * LANES] = e[:main, :]
    for n, (a, b) in enumerate(((e0, e1), (e2, e3))):
        lanes = slice((4 + n) * LANES, (5 + n) * LANES)
        for m in range(EXT):
            x = a[main + m * HALF : main + (m + 1) * HALF, :]
            v = b[main + m * HALF : main + (m + 1) * HALF, :]
            matrix[m * PIECE : m * PIECE + HALF, lanes] = jnp.where(left, x, v)
            matrix[m * PIECE + HALF : (m + 1) * PIECE, lanes] = swap_halves(jnp.where(left, v, x))

    @pl.loop(0, EXT)
    def _(m):
        rows = pl.ds(pl.multiple_of(m * PIECE, PIECE), PIECE)
        out[rows, :] = (dot(matrix[rows, :], factor[...]) * math.sqrt(FACE)).astype(jnp.bfloat16)


def update(ids, chunks, factor):
    vmem = pl.BlockSpec(memory_space=pltpu.VMEM)
    return pl.pallas_call(
        update_kernel,
        in_specs=[pl.BlockSpec(memory_space=pltpu.SMEM)] + [vmem] * 5,
        out_specs=vmem,
        out_shape=jax.ShapeDtypeStruct((EXT * PIECE, FACE), jnp.bfloat16),
        scratch_shapes=[pltpu.VMEM((EXT * PIECE, FACE), jnp.bfloat16)],
        cost_estimate=pl.CostEstimate(flops=1130 * 10**6, bytes_accessed=4 * 10**6, transcendentals=0),
        compiler_params=pltpu.CompilerParams(vmem_limit_bytes=32 * 2**20),
        name="update",
    )(ids, *chunks, factor)


def swap(value, mask):
    pairs = [(source, source ^ mask) for source in range(lax.axis_size("tile"))]
    return lax.ppermute(value, "tile", pairs)


def outward(value):
    pairs = []
    for source in range(lax.axis_size("tile")):
        y = source % 8
        pairs.append((source, source - y + (y + 2 * (y % 2) - 1) % 8))
    return lax.ppermute(value, "tile", pairs)


def to_partner(value):
    return lax.ppermute(value, "pair", [(0, 1), (1, 0)])


def local(child_maps, face_order):
    ids = jnp.stack([lax.axis_index("pair"), lax.axis_index("tile")]).astype(jnp.int32)
    tile, win, ext = extract(child_maps[0, 0], face_order[0], ids)
    y1 = swap(tile, 1)
    e2 = swap(ext, 2)
    w4 = swap(win, 4)
    a0 = jnp.concatenate([tile, y1])
    y2 = outward(a0)
    z1 = swap(jnp.concatenate([a0, win]), 8)
    e1 = swap(ext, 1)
    y3 = swap(y2, 1)
    z2 = swap(jnp.concatenate([y2, w4]), 8)
    y4 = outward(y3)
    z3 = swap(y3, 8)
    px1 = to_partner(jnp.concatenate([a0, win, y2, w4, z1, z2]))
    z4 = swap(y4, 8)
    e3 = swap(ext, 3)
    px2 = to_partner(jnp.concatenate([y3, y4, z3, z4]))
    factor = series(ids, [a0, win, y2, w4, z1, z2, y3, y4, z3, z4, px1, px2])
    return update(ids, [ext, e1, e2, e3], factor)[None, None]


def solution(mesh):
    return jax.shard_map(
        local,
        mesh=mesh,
        in_specs=(P("pair", ("box", "tile"), None, None), P("box", None, None)),
        out_specs=P("pair", ("box", "tile"), None, None),
        check_vma=False,
    )
```

```python
import math

import jax
import jax.numpy as jnp
from jax import lax
from jax.experimental import pallas as pl
from jax.experimental.pallas import tpu as pltpu
from jax.sharding import PartitionSpec as P

FACE = 768
FACES = 6
CF = 2
PIECE = 192
LANES = 128
HALF = PIECE // 2
TILE_ROWS = PIECE + HALF
WIN_ROWS = CF * PIECE * PIECE // LANES
RING = 8
EXT = FACES - 1
EXT_ROWS = EXT * TILE_ROWS
EXT_SHAPE = (EXT_ROWS, LANES)


def ext_store(out, rows, value):
    out[rows, :] = value


def dot(a, b):
    return jnp.dot(a, b, preferred_element_type=jnp.float32)


def one_hot(condition):
    return jnp.where(condition, 1.0, 0.0).astype(jnp.bfloat16)


def packers(shift, odd_col):
    r = lax.broadcasted_iota(jnp.int32, (256, 256), 0)
    c = lax.broadcasted_iota(jnp.int32, (256, 256), 1)
    first = (c < LANES) & (r == c + shift)

    def rest(offset):
        q = c - LANES - offset
        return one_hot(first | ((q >= 0) & (q < 64) & (r == q + LANES + shift)))

    return rest(64 * odd_col), rest(64 * (1 - odd_col))


def pack(ca, cb, starts, shift, odd_col):
    q_top, q_bottom = packers(shift, odd_col)

    def half(offset):
        rows = [pl.ds(pl.multiple_of(start + offset, HALF), HALF) for start in starts]
        return jnp.concatenate([jnp.concatenate([ca[at, :], cb[at, :]], axis=1) for at in rows], axis=0)

    top, bottom = dot(half(0), q_top), dot(half(HALF), q_bottom)
    packed = []
    for m in range(len(starts)):
        rows = slice(m * HALF, (m + 1) * HALF)
        left = jnp.concatenate([top[rows, :LANES], bottom[rows, :LANES]], axis=0)
        packed.append((left.astype(jnp.bfloat16), (top[rows, LANES:] + bottom[rows, LANES:]).astype(jnp.bfloat16)))
    return packed


def here():
    return lax.axis_index("pair"), lax.axis_index("tile")


def shared_kernel(face, ca, cb, out):
    pair, tile = here()
    ((left, rest),) = pack(ca, cb, [0], 64 * (face[pair, 0] & 1), tile & 1)
    for n in range(RING):
        out[n, :PIECE] = left
        out[n, PIECE:] = rest


def edges_kernel(face, ca, cb, w0a, w0b, w1a, w1b, win_out, ext_out):
    pair, tile = here()
    starts = [face[pair, m + 1] * PIECE for m in range(EXT)]
    for m, (left, rest) in enumerate(pack(ca, cb, starts, 64 * (face[pair, 0] & 1), tile & 1)):
        ext_store(ext_out, slice(m * PIECE, (m + 1) * PIECE), left)
        ext_store(ext_out, slice(EXT * PIECE + m * HALF, EXT * PIECE + (m + 1) * HALF), rest)
    r = lax.broadcasted_iota(jnp.int32, (256, CF * PIECE), 0)
    c = lax.broadcasted_iota(jnp.int32, (256, CF * PIECE), 1)
    total = None
    for n, (a, b) in enumerate(((w0a, w0b), (w1a, w1b))):
        q = c - n * PIECE
        move = one_hot((q >= 0) & (q < PIECE) & (r == q + 64 * (face[pair, 1 + n] & 1)))
        part = dot(jnp.concatenate([a[...], b[...]], axis=1), move)
        total = part if total is None else total + part
    for n in range(3):
        win_out[n * PIECE : (n + 1) * PIECE, :] = total[:, n * LANES : (n + 1) * LANES].astype(jnp.bfloat16)


def column(rows, order, step, block):
    def index(g, face):
        faces = face.at[lax.axis_index("pair")]
        return faces[0] if block else 0, (faces[order] * PIECE) // LANES + step

    return pl.BlockSpec((rows, LANES), index)


def extraction(kernel, in_specs, shapes, cost):
    return pl.pallas_call(
        kernel,
        grid_spec=pltpu.PrefetchScalarGridSpec(
            num_scalar_prefetch=1,
            grid=(1,),
            in_specs=in_specs,
            out_specs=[pl.BlockSpec(shape, lambda g, f, d=len(shape): (0,) * d) for shape in shapes],
        ),
        out_shape=[jax.ShapeDtypeStruct(shape, jnp.bfloat16) for shape in shapes],
        cost_estimate=cost,
    )


def extract_shared(tile, face):
    specs = [column(PIECE, 0, step, True) for step in range(2)]
    cost = pl.CostEstimate(flops=3 * 10**7, bytes_accessed=10**6, transcendentals=0)
    return extraction(shared_kernel, specs, [(RING, TILE_ROWS, LANES)], cost)(face, tile, tile)[0]


def extract_edges(tile, face):
    specs = [column(tile.shape[0], 0, step, False) for step in range(2)]
    specs += [column(PIECE, 1 + n, step, True) for n in range(CF) for step in range(2)]
    shapes = [(WIN_ROWS, LANES), EXT_SHAPE]
    cost = pl.CostEstimate(flops=4 * 10**8, bytes_accessed=2 * 10**6, transcendentals=0)
    return extraction(edges_kernel, specs, shapes, cost)(face, *[tile] * 6)


def main_at(index, own_col):
    return pl.multiple_of(LANES * (index ^ own_col), LANES)


def rest_at(index, own_col):
    return pl.multiple_of(4 * LANES + LANES * ((index ^ own_col) >> 1) + 64 * (index & 1), 64)


def swap_halves(x):
    return jnp.concatenate([x[:, 64:], x[:, :64]], axis=1)


def place_tile(source, n, target, rests, row, col, own_col):
    lanes = pl.ds(main_at(col, own_col), LANES)
    target[pl.ds(main_at(row, own_col), LANES), lanes] = source[n, :LANES]
    target[pl.ds(rest_at(row, own_col), 64), lanes] = source[n, LANES:PIECE]
    rests[row, col] = source[n, PIECE:]


def join_rests(target, rests, own_col):
    left = lax.broadcasted_iota(jnp.int32, (HALF, LANES), 1) < 64

    def body(step, carry):
        row, two = step // 2, step % 2
        even, odd = rests[row, 2 * two], rests[row, 2 * two + 1]
        lanes = pl.ds(pl.multiple_of(4 * LANES + LANES * (two ^ (own_col >> 1)), LANES), LANES)
        top = jnp.where(left, even, odd)
        bottom = swap_halves(jnp.where(left, odd, even))
        start = main_at(row, own_col)
        target[pl.ds(start, HALF), lanes] = top
        target[pl.ds(pl.multiple_of(start + HALF, 32), LANES - HALF), lanes] = bottom[: LANES - HALF]
        target[pl.ds(rest_at(row, own_col), 64), lanes] = bottom[LANES - HALF :]
        return carry

    lax.fori_loop(0, 8, body, 0)


def series_kernel(own, far, p_own, p_far, win, w4, zv, zw, pxw, out, *scratch):
    mine, other, rests, power, power2, start_a, total = scratch
    pair, tile = here()
    z = tile >> 3
    own_col = tile & 3
    own_row = tile >> 2

    def place(target, near, far):
        for plane, parts in ((z, near), (1 - z, far)):
            for n in range(RING):
                place_tile(parts, n, target, rests, 2 * plane + n // 4, n % 4, own_col)
        join_rests(target, rests, own_col)

    def place_window(lane_half, sources, target):
        for n, (source, base) in enumerate(sources):
            row = own_row ^ n
            for piece in range(3):
                at = base + piece * PIECE
                lanes = lane_half(piece)
                target[pl.ds(main_at(row, own_col), LANES), lanes] = source[at : at + LANES, :]
                target[pl.ds(rest_at(row, own_col), 64), lanes] = source[at + LANES : at + PIECE, :]

    win_sources = (
        [(x, 0) for x in (win, w4, zv, zw)],
        [(pxw, n * WIN_ROWS) for n in range(4)],
    )
    place(mine, own, far)
    place(other, p_own, p_far)
    half = CF * PIECE
    my_half = pair * half
    place_window(lambda p: pl.ds(p * LANES, LANES), win_sources[0], start_a)
    place_window(lambda p: pl.ds(pl.multiple_of(half - my_half + p * LANES, LANES), LANES), win_sources[1], total)

    lanes = pl.ds(pl.multiple_of(my_half, LANES), half)
    power[...] = dot(other[...], mine[...]).astype(jnp.bfloat16)
    total[:, lanes] = dot(other[...], start_a[...]).astype(jnp.bfloat16)

    def add(matrix, source, target):
        target[...] = (source[...].astype(jnp.float32) + dot(matrix[...], source[...])).astype(jnp.bfloat16)

    power2[...] = dot(power[...], power[...]).astype(jnp.bfloat16)
    add(power, total, mine)
    add(power2, mine, other)
    power[...] = dot(power2[...], power2[...]).astype(jnp.bfloat16)
    add(power, other, out)


def series(lists):
    vmem = pl.BlockSpec(memory_space=pltpu.VMEM)
    square = pltpu.VMEM((FACE, FACE), jnp.bfloat16)
    return pl.pallas_call(
        series_kernel,
        in_specs=[vmem] * len(lists),
        out_specs=vmem,
        out_shape=jax.ShapeDtypeStruct((FACE, FACE), jnp.bfloat16),
        scratch_shapes=[
            square,
            square,
            pltpu.VMEM((4, 4, HALF, LANES), jnp.bfloat16),
            square,
            square,
            pltpu.VMEM((FACE, CF * PIECE), jnp.bfloat16),
            square,
        ],
        cost_estimate=pl.CostEstimate(flops=6 * 10**9, bytes_accessed=6 * 10**6, transcendentals=0),
        compiler_params=pltpu.CompilerParams(vmem_limit_bytes=40 * 2**20),
        name="series",
    )(*lists)


def update_kernel(e0, e1, e2, near, relayed, factor, out, matrix):
    col = here()[1] & 3
    inner = ((col ^ (col >> 1)) & 1) == 1
    left = (lax.broadcasted_iota(jnp.int32, (HALF, LANES), 1) < 64) ^ ((col & 1) == 1)
    main = EXT * PIECE

    def fill(two, a, b):
        for n, e in enumerate((a, b)):
            matrix[:, (2 * two + n) * LANES : (2 * two + n + 1) * LANES] = e[:main, :]
        lanes = slice((4 + two) * LANES, (5 + two) * LANES)
        for m in range(EXT):
            x = a[main + m * HALF : main + (m + 1) * HALF, :]
            v = b[main + m * HALF : main + (m + 1) * HALF, :]
            matrix[m * PIECE : m * PIECE + HALF, lanes] = jnp.where(left, x, v)
            matrix[m * PIECE + HALF : (m + 1) * PIECE, lanes] = swap_halves(jnp.where(left, v, x))

    fill(0, e0, e1)

    @pl.when(inner)
    def _():
        fill(1, e2, near)

    @pl.when(jnp.logical_not(inner))
    def _():
        fill(1, e2, relayed)

    for m in range(2):
        rows = slice(m * main // 2, (m + 1) * main // 2)
        out[rows, :] = (dot(matrix[rows, :], factor[...]) * math.sqrt(FACE)).astype(jnp.bfloat16)


def update(chunks, factor):
    vmem = pl.BlockSpec(memory_space=pltpu.VMEM)
    return pl.pallas_call(
        update_kernel,
        in_specs=[vmem] * (len(chunks) + 1),
        out_specs=vmem,
        out_shape=jax.ShapeDtypeStruct((EXT * PIECE, FACE), jnp.bfloat16),
        scratch_shapes=[pltpu.VMEM((EXT * PIECE, FACE), jnp.bfloat16)],
        cost_estimate=pl.CostEstimate(flops=1130 * 10**6, bytes_accessed=4 * 10**6, transcendentals=0),
        compiler_params=pltpu.CompilerParams(vmem_limit_bytes=32 * 2**20),
        name="update",
    )(*chunks, factor)


def permute(value, pairs, axis="tile"):
    return lax.ppermute(value, axis, pairs)


def masked(mask):
    return [(source, source ^ mask) for source in range(16)]


def ring_gather(copies):
    groups = [[RING * z + y for y in range(RING)] for z in range(2)]
    return lax.all_to_all(copies, "tile", 0, 0, axis_index_groups=groups, tiled=True)


def in_rows(steps):
    return [(4 * row + a, 4 * row + b) for row in range(4) for a, b in steps]


def program(child_maps, face_order):
    inner, outer = in_rows(((1, 2), (2, 1))), in_rows(((1, 0), (2, 3)))
    partner = [(0, 1), (1, 0)]
    own = ring_gather(extract_shared(child_maps[0, 0], face_order[0]))
    win, ext = extract_edges(child_maps[0, 0], face_order[0])
    w4 = permute(win, masked(4))
    e2 = permute(ext, masked(2))
    zv = permute(win, masked(8))
    zw = permute(w4, masked(8))
    e1 = permute(ext, masked(1))
    pxw = permute(jnp.concatenate([win, w4, zv, zw]), partner, "pair")
    far = permute(own, masked(8))
    p_own = permute(own, partner, "pair")
    p_far = permute(far, partner, "pair")
    near = permute(ext, inner)
    relayed = permute(e2, outer)
    factor = series([own, far, p_own, p_far, win, w4, zv, zw, pxw])
    return update([ext, e1, e2, near, relayed], factor)[None, None]


def solution(mesh):
    return jax.shard_map(
        program,
        mesh=mesh,
        in_specs=(P("pair", ("box", "tile"), None, None), P("box", None, None)),
        out_specs=P("pair", ("box", "tile"), None, None),
        check_vma=False,
    )
```

```python
import math

import jax
import jax.numpy as jnp
from jax import lax
from jax.experimental import pallas as pl
from jax.experimental.pallas import tpu as pltpu
from jax.sharding import PartitionSpec as P

FACE = 768
FACES = 6
CF = 2
PIECE = 192
LANES = 128
HALF = PIECE // 2
TILE_ROWS = PIECE + HALF
WIN_ROWS = CF * PIECE * PIECE // LANES
RING = 8
EXT = FACES - 1
EXT_ROWS = EXT * TILE_ROWS
EXT_SHAPE = (EXT_ROWS, LANES)


def ext_store(out, rows, value):
    out[rows, :] = value


def dot(a, b):
    return jnp.dot(a, b, preferred_element_type=jnp.float32)


def one_hot(condition):
    return jnp.where(condition, 1.0, 0.0).astype(jnp.bfloat16)


def packers(shift, odd_col):
    r = lax.broadcasted_iota(jnp.int32, (256, 256), 0)
    c = lax.broadcasted_iota(jnp.int32, (256, 256), 1)
    first = (c < LANES) & (r == c + shift)

    def rest(offset):
        q = c - LANES - offset
        return one_hot(first | ((q >= 0) & (q < 64) & (r == q + LANES + shift)))

    return rest(64 * odd_col), rest(64 * (1 - odd_col))


def pack(ca, cb, starts, shift, odd_col):
    q_top, q_bottom = packers(shift, odd_col)

    def half(offset):
        rows = [pl.ds(pl.multiple_of(start + offset, HALF), HALF) for start in starts]
        return jnp.concatenate([jnp.concatenate([ca[at, :], cb[at, :]], axis=1) for at in rows], axis=0)

    top, bottom = dot(half(0), q_top), dot(half(HALF), q_bottom)
    packed = []
    for m in range(len(starts)):
        rows = slice(m * HALF, (m + 1) * HALF)
        left = jnp.concatenate([top[rows, :LANES], bottom[rows, :LANES]], axis=0)
        packed.append((left.astype(jnp.bfloat16), (top[rows, LANES:] + bottom[rows, LANES:]).astype(jnp.bfloat16)))
    return packed


def here():
    return lax.axis_index("pair"), lax.axis_index("tile")


def shared_kernel(face, ca, cb, out):
    pair, tile = here()
    ((left, rest),) = pack(ca, cb, [0], 64 * (face[pair, 0] & 1), tile & 1)
    for n in range(RING):
        out[n, :PIECE] = left
        out[n, PIECE:] = rest


def edges_kernel(face, ca, cb, w0a, w0b, w1a, w1b, win_out, ext_out):
    pair, tile = here()
    starts = [face[pair, m + 1] * PIECE for m in range(EXT)]
    for m, (left, rest) in enumerate(pack(ca, cb, starts, 64 * (face[pair, 0] & 1), tile & 1)):
        ext_store(ext_out, slice(m * PIECE, (m + 1) * PIECE), left)
        ext_store(ext_out, slice(EXT * PIECE + m * HALF, EXT * PIECE + (m + 1) * HALF), rest)
    r = lax.broadcasted_iota(jnp.int32, (256, CF * PIECE), 0)
    c = lax.broadcasted_iota(jnp.int32, (256, CF * PIECE), 1)
    total = None
    for n, (a, b) in enumerate(((w0a, w0b), (w1a, w1b))):
        q = c - n * PIECE
        move = one_hot((q >= 0) & (q < PIECE) & (r == q + 64 * (face[pair, 1 + n] & 1)))
        part = dot(jnp.concatenate([a[...], b[...]], axis=1), move)
        total = part if total is None else total + part
    for n in range(3):
        win_out[n * PIECE : (n + 1) * PIECE, :] = total[:, n * LANES : (n + 1) * LANES].astype(jnp.bfloat16)


def column(rows, order, step, block):
    def index(g, face):
        faces = face.at[lax.axis_index("pair")]
        return faces[0] if block else 0, (faces[order] * PIECE) // LANES + step

    return pl.BlockSpec((rows, LANES), index)


def extraction(kernel, in_specs, shapes, cost):
    return pl.pallas_call(
        kernel,
        grid_spec=pltpu.PrefetchScalarGridSpec(
            num_scalar_prefetch=1,
            grid=(1,),
            in_specs=in_specs,
            out_specs=[pl.BlockSpec(shape, lambda g, f, d=len(shape): (0,) * d) for shape in shapes],
        ),
        out_shape=[jax.ShapeDtypeStruct(shape, jnp.bfloat16) for shape in shapes],
        cost_estimate=cost,
    )


def extract_shared(tile, face):
    specs = [column(PIECE, 0, step, True) for step in range(2)]
    cost = pl.CostEstimate(flops=3 * 10**7, bytes_accessed=10**6, transcendentals=0)
    return extraction(shared_kernel, specs, [(RING, TILE_ROWS, LANES)], cost)(face, tile, tile)[0]


def extract_edges(tile, face):
    specs = [column(tile.shape[0], 0, step, False) for step in range(2)]
    specs += [column(PIECE, 1 + n, step, True) for n in range(CF) for step in range(2)]
    shapes = [(WIN_ROWS, LANES), EXT_SHAPE]
    cost = pl.CostEstimate(flops=4 * 10**8, bytes_accessed=2 * 10**6, transcendentals=0)
    return extraction(edges_kernel, specs, shapes, cost)(face, *[tile] * 6)


def main_at(index, own_col):
    return pl.multiple_of(LANES * (index ^ own_col), LANES)


def rest_at(index, own_col):
    return pl.multiple_of(4 * LANES + LANES * ((index ^ own_col) >> 1) + 64 * (index & 1), 64)


def swap_halves(x):
    return jnp.concatenate([x[:, 64:], x[:, :64]], axis=1)


def place_tile(source, n, target, rests, row, col, own_col):
    lanes = pl.ds(main_at(col, own_col), LANES)
    base = n * TILE_ROWS
    target[pl.ds(main_at(row, own_col), LANES), lanes] = source[base : base + LANES, :]
    target[pl.ds(rest_at(row, own_col), 64), lanes] = source[base + LANES : base + PIECE, :]
    rests[row, col] = source[base + PIECE : base + TILE_ROWS, :]


def join_rests(target, rests, own_col):
    left = lax.broadcasted_iota(jnp.int32, (HALF, LANES), 1) < 64

    def body(step, carry):
        row, two = step // 2, step % 2
        even, odd = rests[row, 2 * two], rests[row, 2 * two + 1]
        lanes = pl.ds(pl.multiple_of(4 * LANES + LANES * (two ^ (own_col >> 1)), LANES), LANES)
        top = jnp.where(left, even, odd)
        bottom = swap_halves(jnp.where(left, odd, even))
        start = main_at(row, own_col)
        target[pl.ds(start, HALF), lanes] = top
        target[pl.ds(pl.multiple_of(start + HALF, 32), LANES - HALF), lanes] = bottom[: LANES - HALF]
        target[pl.ds(rest_at(row, own_col), 64), lanes] = bottom[LANES - HALF :]
        return carry

    lax.fori_loop(0, 8, body, 0)


def series_kernel(own, far, p_own, p_far, win, w4, zv, zw, out, *scratch):
    mine, other, rests, power, power2, start_a, total = scratch
    pair, tile = here()
    z = tile >> 3
    own_col = tile & 3
    own_row = tile >> 2

    def place(target, near, far):
        for plane, parts in ((z, near), (1 - z, far)):
            for n in range(RING):
                place_tile(parts, n, target, rests, 2 * plane + n // 4, n % 4, own_col)
        join_rests(target, rests, own_col)

    def place_window(lane_half, sources, target):
        for n, (source, base) in enumerate(sources):
            row = own_row ^ n
            for piece in range(3):
                at = base + piece * PIECE
                lanes = lane_half(piece)
                target[pl.ds(main_at(row, own_col), LANES), lanes] = source[at : at + LANES, :]
                target[pl.ds(rest_at(row, own_col), 64), lanes] = source[at + LANES : at + PIECE, :]

    base = RING * TILE_ROWS
    win_sources = (
        [(x, 0) for x in (win, w4, zv, zw)],
        [(x, base + n * WIN_ROWS) for n, x in ((0, p_own), (0, p_far), (1, p_own), (1, p_far))],
    )
    place(mine, own, far)
    place(other, p_own, p_far)
    half = CF * PIECE
    my_half = pair * half
    place_window(lambda p: pl.ds(p * LANES, LANES), win_sources[0], start_a)
    place_window(lambda p: pl.ds(pl.multiple_of(half - my_half + p * LANES, LANES), LANES), win_sources[1], total)

    lanes = pl.ds(pl.multiple_of(my_half, LANES), half)
    power[...] = dot(other[...], mine[...]).astype(jnp.bfloat16)
    total[:, lanes] = dot(other[...], start_a[...]).astype(jnp.bfloat16)

    def add(matrix, source, target):
        target[...] = (source[...].astype(jnp.float32) + dot(matrix[...], source[...])).astype(jnp.bfloat16)

    power2[...] = dot(power[...], power[...]).astype(jnp.bfloat16)
    add(power, total, mine)
    add(power2, mine, other)
    power[...] = dot(power2[...], power2[...]).astype(jnp.bfloat16)
    add(power, other, out)


def series(lists):
    vmem = pl.BlockSpec(memory_space=pltpu.VMEM)
    square = pltpu.VMEM((FACE, FACE), jnp.bfloat16)
    return pl.pallas_call(
        series_kernel,
        in_specs=[vmem] * len(lists),
        out_specs=vmem,
        out_shape=jax.ShapeDtypeStruct((FACE, FACE), jnp.bfloat16),
        scratch_shapes=[
            square,
            square,
            pltpu.VMEM((4, 4, HALF, LANES), jnp.bfloat16),
            square,
            square,
            pltpu.VMEM((FACE, CF * PIECE), jnp.bfloat16),
            square,
        ],
        cost_estimate=pl.CostEstimate(flops=6 * 10**9, bytes_accessed=6 * 10**6, transcendentals=0),
        compiler_params=pltpu.CompilerParams(vmem_limit_bytes=40 * 2**20),
        name="series",
    )(*lists)


def update_kernel(e0, e1, to_inner, to_outer, near, relayed, factor, out, matrix, held, done):
    col = here()[1] & 3
    inner = ((col ^ (col >> 1)) & 1) == 1
    left = (lax.broadcasted_iota(jnp.int32, (HALF, LANES), 1) < 64) ^ ((col & 1) == 1)
    main = EXT * PIECE

    def fill(two, a, b):
        for n, e in enumerate((a, b)):
            matrix[:, (2 * two + n) * LANES : (2 * two + n + 1) * LANES] = e[:main, :]
        lanes = slice((4 + two) * LANES, (5 + two) * LANES)
        for m in range(EXT):
            x = a[main + m * HALF : main + (m + 1) * HALF, :]
            v = b[main + m * HALF : main + (m + 1) * HALF, :]
            matrix[m * PIECE : m * PIECE + HALF, lanes] = jnp.where(left, x, v)
            matrix[m * PIECE + HALF : (m + 1) * PIECE, lanes] = swap_halves(jnp.where(left, v, x))

    fill(0, e0, e1)

    @pl.when(inner)
    def _():
        fill(1, to_inner, near)

    @pl.when(jnp.logical_not(inner))
    def _():
        fill(1, to_outer, relayed)

    copies = []
    for m in range(2):
        rows = slice(m * main // 2, (m + 1) * main // 2)
        held[rows, :] = (dot(matrix[rows, :], factor[...]) * math.sqrt(FACE)).astype(jnp.bfloat16)
        copies.append(pltpu.make_async_copy(held.at[rows, :], out.at[rows, :], done.at[m]))
        copies[-1].start()
    for copy in copies:
        copy.wait()


def update(chunks, factor):
    vmem = pl.BlockSpec(memory_space=pltpu.VMEM)
    return pl.pallas_call(
        update_kernel,
        in_specs=[vmem] * (len(chunks) + 1),
        out_specs=pl.BlockSpec(memory_space=pl.ANY),
        out_shape=jax.ShapeDtypeStruct((EXT * PIECE, FACE), jnp.bfloat16),
        scratch_shapes=[pltpu.VMEM((EXT * PIECE, FACE), jnp.bfloat16)] * 2 + [pltpu.SemaphoreType.DMA((2,))],
        cost_estimate=pl.CostEstimate(flops=1130 * 10**6, bytes_accessed=4 * 10**6, transcendentals=0),
        compiler_params=pltpu.CompilerParams(vmem_limit_bytes=32 * 2**20),
        name="update",
    )(*chunks, factor)


def permute(value, pairs, axis="tile"):
    return lax.ppermute(value, axis, pairs)


def masked(mask):
    return [(source, source ^ mask) for source in range(16)]


def ring_gather(copies):
    groups = [[RING * z + y for y in range(RING)] for z in range(2)]
    return lax.all_to_all(copies, "tile", 0, 0, axis_index_groups=groups, tiled=True)


def in_rows(steps):
    return [(4 * row + a, 4 * row + b) for row in range(4) for a, b in steps]


def program(child_maps, face_order):
    inner, outer = in_rows(((1, 2), (2, 1))), in_rows(((1, 0), (2, 3)))
    partner = [(0, 1), (1, 0)]
    own = ring_gather(extract_shared(child_maps[0, 0], face_order[0]))
    win, ext = extract_edges(child_maps[0, 0], face_order[0])
    w4 = permute(win, masked(4))
    to_inner = permute(ext, in_rows(((0, 2), (3, 1))))
    to_outer = permute(ext, in_rows(((2, 0), (1, 3))))
    zv = permute(win, masked(8))
    zw = permute(w4, masked(8))
    e1 = permute(ext, masked(1))
    far = permute(own, masked(8))
    flat = (RING * TILE_ROWS, LANES)
    pa = permute(jnp.concatenate([own.reshape(flat), win, zv]), partner, "pair")
    pb = permute(jnp.concatenate([far.reshape(flat), w4, zw]), partner, "pair")
    near = permute(ext, inner)
    relayed = permute(to_inner, outer)
    factor = series([own.reshape(flat), far.reshape(flat), pa, pb, win, w4, zv, zw])
    return update([ext, e1, to_inner, to_outer, near, relayed], factor)[None, None]


def solution(mesh):
    return jax.shard_map(
        program,
        mesh=mesh,
        in_specs=(P("pair", ("box", "tile"), None, None), P("box", None, None)),
        out_specs=P("pair", ("box", "tile"), None, None),
        check_vma=False,
    )
```

```python
import math

import jax
import jax.numpy as jnp
from jax import lax
from jax.experimental import pallas as pl
from jax.experimental.pallas import tpu as pltpu
from jax.sharding import PartitionSpec as P

FACE = 768
FACES = 6
CF = 2
PIECE = 192
LANES = 128
HALF = PIECE // 2
TILE_ROWS = PIECE + HALF
WIN_ROWS = CF * PIECE * PIECE // LANES
RING = 8
EXT = FACES - 1
EXT_ROWS = EXT * TILE_ROWS
EXT_SHAPE = (EXT_ROWS, LANES)


def ext_store(out, rows, value):
    out[rows, :] = value


def dot(a, b):
    return jnp.dot(a, b, preferred_element_type=jnp.float32)


def one_hot(condition):
    return jnp.where(condition, 1.0, 0.0).astype(jnp.bfloat16)


def packers(shift, odd_col):
    r = lax.broadcasted_iota(jnp.int32, (256, 256), 0)
    c = lax.broadcasted_iota(jnp.int32, (256, 256), 1)
    first = (c < LANES) & (r == c + shift)

    def rest(offset):
        q = c - LANES - offset
        return one_hot(first | ((q >= 0) & (q < 64) & (r == q + LANES + shift)))

    return rest(64 * odd_col), rest(64 * (1 - odd_col))


def pack(ca, cb, starts, shift, odd_col):
    q_top, q_bottom = packers(shift, odd_col)

    def half(offset):
        rows = [pl.ds(pl.multiple_of(start + offset, HALF), HALF) for start in starts]
        return jnp.concatenate([jnp.concatenate([ca[at, :], cb[at, :]], axis=1) for at in rows], axis=0)

    top, bottom = dot(half(0), q_top), dot(half(HALF), q_bottom)
    packed = []
    for m in range(len(starts)):
        rows = slice(m * HALF, (m + 1) * HALF)
        left = jnp.concatenate([top[rows, :LANES], bottom[rows, :LANES]], axis=0)
        packed.append((left.astype(jnp.bfloat16), (top[rows, LANES:] + bottom[rows, LANES:]).astype(jnp.bfloat16)))
    return packed


def here():
    return lax.axis_index("pair"), lax.axis_index("tile")


def shared_kernel(face, ca, cb, out):
    pair, tile = here()
    ((left, rest),) = pack(ca, cb, [0], 64 * (face[pair, 0] & 1), tile & 1)
    for n in range(RING):
        out[n, :PIECE] = left
        out[n, PIECE:] = rest


def edges_kernel(face, ca, cb, w0a, w0b, w1a, w1b, win_out, ext_out):
    pair, tile = here()
    starts = [face[pair, m + 1] * PIECE for m in range(EXT)]
    for m, (left, rest) in enumerate(pack(ca, cb, starts, 64 * (face[pair, 0] & 1), tile & 1)):
        ext_store(ext_out, slice(m * PIECE, (m + 1) * PIECE), left)
        ext_store(ext_out, slice(EXT * PIECE + m * HALF, EXT * PIECE + (m + 1) * HALF), rest)
    r = lax.broadcasted_iota(jnp.int32, (256, CF * PIECE), 0)
    c = lax.broadcasted_iota(jnp.int32, (256, CF * PIECE), 1)
    total = None
    for n, (a, b) in enumerate(((w0a, w0b), (w1a, w1b))):
        q = c - n * PIECE
        move = one_hot((q >= 0) & (q < PIECE) & (r == q + 64 * (face[pair, 1 + n] & 1)))
        part = dot(jnp.concatenate([a[...], b[...]], axis=1), move)
        total = part if total is None else total + part
    for n in range(3):
        win_out[n * PIECE : (n + 1) * PIECE, :] = total[:, n * LANES : (n + 1) * LANES].astype(jnp.bfloat16)


def column(rows, order, step, block):
    def index(g, face):
        faces = face.at[lax.axis_index("pair")]
        return faces[0] if block else 0, (faces[order] * PIECE) // LANES + step

    return pl.BlockSpec((rows, LANES), index)


def extraction(kernel, in_specs, shapes, cost):
    return pl.pallas_call(
        kernel,
        grid_spec=pltpu.PrefetchScalarGridSpec(
            num_scalar_prefetch=1,
            grid=(1,),
            in_specs=in_specs,
            out_specs=[pl.BlockSpec(shape, lambda g, f, d=len(shape): (0,) * d) for shape in shapes],
        ),
        out_shape=[jax.ShapeDtypeStruct(shape, jnp.bfloat16) for shape in shapes],
        cost_estimate=cost,
    )


def extract_shared(tile, face):
    specs = [column(PIECE, 0, step, True) for step in range(2)]
    cost = pl.CostEstimate(flops=3 * 10**7, bytes_accessed=10**6, transcendentals=0)
    return extraction(shared_kernel, specs, [(RING, TILE_ROWS, LANES)], cost)(face, tile, tile)[0]


def extract_edges(tile, face):
    specs = [column(tile.shape[0], 0, step, False) for step in range(2)]
    specs += [column(PIECE, 1 + n, step, True) for n in range(CF) for step in range(2)]
    shapes = [(WIN_ROWS, LANES), EXT_SHAPE]
    cost = pl.CostEstimate(flops=4 * 10**8, bytes_accessed=2 * 10**6, transcendentals=0)
    return extraction(edges_kernel, specs, shapes, cost)(face, *[tile] * 6)


def main_at(index, own_col):
    return pl.multiple_of(LANES * (index ^ own_col), LANES)


def rest_at(index, own_col):
    return pl.multiple_of(4 * LANES + LANES * ((index ^ own_col) >> 1) + 64 * (index & 1), 64)


def swap_halves(x):
    return jnp.concatenate([x[:, 64:], x[:, :64]], axis=1)


PLANE = FACE // 2


def store_tile(source, n, target, rests, main, rest, row, col, own_col):
    base = n * TILE_ROWS
    lanes = pl.ds(main_at(col, own_col), LANES)
    target[pl.ds(main, LANES), lanes] = source[base : base + LANES, :]
    target[pl.ds(rest, 64), lanes] = source[base + LANES : base + PIECE, :]
    rests[row, col] = source[base + PIECE : base + TILE_ROWS, :]


def join_rests(target, rests, places, own_col):
    left = lax.broadcasted_iota(jnp.int32, (HALF, LANES), 1) < 64
    for row, (main, rest) in enumerate(places):
        for two in range(2):
            even, odd = rests[row, 2 * two], rests[row, 2 * two + 1]
            lanes = pl.ds(pl.multiple_of(4 * LANES + LANES * (two ^ (own_col >> 1)), LANES), LANES)
            bottom = swap_halves(jnp.where(left, odd, even))
            target[pl.ds(main, HALF), lanes] = jnp.where(left, even, odd)
            target[pl.ds(pl.multiple_of(main + HALF, 32), LANES - HALF), lanes] = bottom[: LANES - HALF]
            target[pl.ds(rest, 64), lanes] = bottom[LANES - HALF :]


def place_plane(tiles, target, rests, own_col):
    places = [(pl.multiple_of(LANES * (row ^ (own_col & 1)), LANES), 2 * LANES + 64 * row) for row in range(2)]
    for n in range(RING):
        store_tile(tiles, n, target, rests, *places[n // 4], n // 4, n % 4, own_col)
    join_rests(target, rests, places, own_col)


def plane_rows(plane, own_col):
    q = plane ^ (own_col >> 1)
    return pl.ds(pl.multiple_of(2 * LANES * q, 2 * LANES), 2 * LANES), pl.ds(
        pl.multiple_of(4 * LANES + LANES * q, LANES), LANES
    )


def place_window(lane_half, sources, target, own_row, own_col):
    for n, (source, base) in enumerate(sources):
        row = own_row ^ n
        for piece in range(3):
            at = base + piece * PIECE
            lanes = lane_half(piece)
            target[pl.ds(main_at(row, own_col), LANES), lanes] = source[at : at + LANES, :]
            target[pl.ds(rest_at(row, own_col), 64), lanes] = source[at + LANES : at + PIECE, :]


def prepare_kernel(own, far, p_own, early, w4, zw, mine, half_power, half_start, start_a, half, rests):
    tile = here()[1]
    z = tile >> 3
    own_col = tile & 3
    own_row = tile >> 2
    for plane, tiles in ((z, own), (1 - z, far)):
        places = [(main_at(2 * plane + n, own_col), rest_at(2 * plane + n, own_col)) for n in range(2)]
        for n in range(RING):
            store_tile(tiles, n, mine, rests, *places[n // 4], n // 4, n % 4, own_col)
        join_rests(mine, rests, places, own_col)
    place_plane(p_own, half, rests, own_col)

    sources = [(early, 0), (w4, 0), (early, WIN_ROWS), (zw, 0)]
    place_window(lambda p: pl.ds(p * LANES, LANES), sources, start_a, own_row, own_col)
    half_power[...] = dot(half[...], mine[...]).astype(jnp.bfloat16)
    half_start[...] = dot(half[...], start_a[...]).astype(jnp.bfloat16)


def series_kernel(p_own, p_far, mine, half_power, half_start, start_a, out, half, rests, power, power2, total, next_):
    pair, tile = here()
    z = tile >> 3
    own_col = tile & 3
    width = CF * PIECE
    lanes = pl.ds(pl.multiple_of(pair * width, LANES), width)
    place_plane(p_far, half, rests, own_col)
    base = RING * TILE_ROWS
    theirs = [(x, base + n * WIN_ROWS) for n in range(2) for x in (p_own, p_far)]
    place_window(
        lambda p: pl.ds(pl.multiple_of(width - pair * width + p * LANES, LANES), LANES), theirs, total, tile >> 2, own_col
    )

    def spread(plane, powers, starts):
        main, rest = plane_rows(plane, own_col)
        for rows, part in ((main, slice(0, 2 * LANES)), (rest, slice(2 * LANES, PLANE))):
            power[rows, :] = powers[part, :]
            total[rows, lanes] = starts[part, :]

    spread(z, half_power, half_start)
    spread(
        1 - z,
        dot(half[...], mine[...]).astype(jnp.bfloat16),
        dot(half[...], start_a[...]).astype(jnp.bfloat16),
    )

    def add(matrix, source, target):
        target[...] = (source[...].astype(jnp.float32) + dot(matrix[...], source[...])).astype(jnp.bfloat16)

    power2[...] = dot(power[...], power[...]).astype(jnp.bfloat16)
    add(power, total, next_)
    add(power2, next_, total)
    power[...] = dot(power2[...], power2[...]).astype(jnp.bfloat16)
    add(power, total, out)


def in_vmem(kernel, args, outs, scratch, flops):
    vmem = pl.BlockSpec(memory_space=pltpu.VMEM)
    return pl.pallas_call(
        kernel,
        in_specs=[vmem] * len(args),
        out_specs=[vmem] * len(outs),
        out_shape=[jax.ShapeDtypeStruct(shape, jnp.bfloat16) for shape in outs],
        scratch_shapes=[pltpu.VMEM(shape, jnp.bfloat16) for shape in scratch],
        cost_estimate=pl.CostEstimate(flops=flops, bytes_accessed=4 * 10**6, transcendentals=0),
        compiler_params=pltpu.CompilerParams(vmem_limit_bytes=32 * 2**20),
    )(*args)


SQUARE = (FACE, FACE)
RESTS = (2, 4, HALF, LANES)


def prepare(*args):
    outs = [SQUARE, (PLANE, FACE), (PLANE, CF * PIECE), (FACE, CF * PIECE)]
    return in_vmem(prepare_kernel, args, outs, [(PLANE, FACE), RESTS], 7 * 10**8)


def series(*args):
    return in_vmem(series_kernel, args, [SQUARE], [(PLANE, FACE), RESTS] + [SQUARE] * 4, 5 * 10**9)[0]


def update_kernel(e0, e1, to_inner, to_outer, near, relayed, factor, out, matrix, held, done):
    col = here()[1] & 3
    inner = ((col ^ (col >> 1)) & 1) == 1
    left = (lax.broadcasted_iota(jnp.int32, (HALF, LANES), 1) < 64) ^ ((col & 1) == 1)
    main = EXT * PIECE

    def fill(two, a, b):
        for n, e in enumerate((a, b)):
            matrix[:, (2 * two + n) * LANES : (2 * two + n + 1) * LANES] = e[:main, :]
        lanes = slice((4 + two) * LANES, (5 + two) * LANES)
        for m in range(EXT):
            x = a[main + m * HALF : main + (m + 1) * HALF, :]
            v = b[main + m * HALF : main + (m + 1) * HALF, :]
            matrix[m * PIECE : m * PIECE + HALF, lanes] = jnp.where(left, x, v)
            matrix[m * PIECE + HALF : (m + 1) * PIECE, lanes] = swap_halves(jnp.where(left, v, x))

    fill(0, e0, e1)

    @pl.when(inner)
    def _():
        fill(1, to_inner, near)

    @pl.when(jnp.logical_not(inner))
    def _():
        fill(1, to_outer, relayed)

    copies = []
    for m in range(2):
        rows = slice(m * main // 2, (m + 1) * main // 2)
        held[rows, :] = (dot(matrix[rows, :], factor[...]) * math.sqrt(FACE)).astype(jnp.bfloat16)
        copies.append(pltpu.make_async_copy(held.at[rows, :], out.at[rows, :], done.at[m]))
        copies[-1].start()
    for copy in copies:
        copy.wait()


def update(chunks, factor):
    vmem = pl.BlockSpec(memory_space=pltpu.VMEM)
    return pl.pallas_call(
        update_kernel,
        in_specs=[vmem] * (len(chunks) + 1),
        out_specs=pl.BlockSpec(memory_space=pl.ANY),
        out_shape=jax.ShapeDtypeStruct((EXT * PIECE, FACE), jnp.bfloat16),
        scratch_shapes=[pltpu.VMEM((EXT * PIECE, FACE), jnp.bfloat16)] * 2 + [pltpu.SemaphoreType.DMA((2,))],
        cost_estimate=pl.CostEstimate(flops=1130 * 10**6, bytes_accessed=4 * 10**6, transcendentals=0),
        compiler_params=pltpu.CompilerParams(vmem_limit_bytes=32 * 2**20),
        name="update",
    )(*chunks, factor)


def permute(value, pairs, axis="tile"):
    return lax.ppermute(value, axis, pairs)


def masked(mask):
    return [(source, source ^ mask) for source in range(16)]


def ring_gather(copies):
    groups = [[RING * z + y for y in range(RING)] for z in range(2)]
    return lax.all_to_all(copies, "tile", 0, 0, axis_index_groups=groups, tiled=True)


def in_rows(steps):
    return [(4 * row + a, 4 * row + b) for row in range(4) for a, b in steps]


def program(child_maps, face_order):
    inner, outer = in_rows(((1, 2), (2, 1))), in_rows(((1, 0), (2, 3)))
    partner = [(0, 1), (1, 0)]
    own = ring_gather(extract_shared(child_maps[0, 0], face_order[0]))
    win, ext = extract_edges(child_maps[0, 0], face_order[0])
    w4 = permute(win, masked(4))
    to_inner = permute(ext, in_rows(((0, 2), (3, 1))))
    to_outer = permute(ext, in_rows(((2, 0), (1, 3))))
    zv = permute(win, masked(8))
    zw = permute(w4, masked(8))
    e1 = permute(ext, masked(1))
    far = permute(own, masked(8))
    flat = (RING * TILE_ROWS, LANES)
    early = lax.optimization_barrier(jnp.concatenate([win, zv]))
    pa = permute(jnp.concatenate([own.reshape(flat), early]), partner, "pair")
    pb = permute(jnp.concatenate([far.reshape(flat), w4, zw]), partner, "pair")
    near = permute(ext, inner)
    relayed = permute(to_inner, outer)
    ready = prepare(own.reshape(flat), far.reshape(flat), pa, early, w4, zw)
    factor = series(pa, pb, *ready)
    return update([ext, e1, to_inner, to_outer, near, relayed], factor)[None, None]


def solution(mesh):
    return jax.shard_map(
        program,
        mesh=mesh,
        in_specs=(P("pair", ("box", "tile"), None, None), P("box", None, None)),
        out_specs=P("pair", ("box", "tile"), None, None),
        check_vma=False,
    )
```
